32 devices in a mesh: segment: 4 (over y, x), dom: 8 (over z, core).
Axes of the slice: x: 2, y: 2, z: 4, core: 2. Of those that a mesh axis runs over, the one named last changes fastest.
Arguments:
- forward_held: float32 [4, 2048, 512], P('segment', 'dom'), may hold values from -6 to 6
- forward_new: float32 [2048, 512], P('dom'), may hold values from -6 to 6
- back_outputs: float32 [4, 2048, 512], P('segment', 'dom'), may hold values from -6 to 6
- back_cotangents: float32 [4, 2048, 512], P('segment', 'dom'), may hold values from -6 to 6
- back_new_outputs: float32 [2048, 512], P('dom'), may hold values from -6 to 6
- back_new_cotangents: float32 [2048, 512], P('dom'), may hold values from -6 to 6
- adj_tiles: float32 [16, 16, 128, 128], P('dom'), may hold values from 0 to 0.046875, as said below
- tile_cols: int32 [16, 16], P('dom'), may hold values from 0 to 15, as said below
- weight_first: float32 [8, 256, 256], P('segment'), may hold values from -0.375 to 0.375
- weight_second: float32 [8, 256, 256], P('segment'), may hold values from -0.375 to 0.375
- gain_first: float32 [8, 256], P('segment'), may hold values from 0.1 to 1.9
- gain_second: float32 [8, 256], P('segment'), may hold values from 0.1 to 1.9
Outputs:
- forward_one: float32 [4, 2048, 512], P('segment', 'dom')
- forward_two: float32 [4, 2048, 512], P('segment', 'dom')
- inputs_one: float32 [4, 2048, 512], P('segment', 'dom')
- cotan_one: float32 [4, 2048, 512], P('segment', 'dom')
- inputs_two: float32 [4, 2048, 512], P('segment', 'dom')
- cotan_two: float32 [4, 2048, 512], P('segment', 'dom')
- grad_weight_first: float32 [8, 256, 256], P('segment')
- grad_weight_second: float32 [8, 256, 256], P('segment')
- grad_gain_first: float32 [8, 256], P('segment')
- grad_gain_second: float32 [8, 256], P('segment')
The draws below stay inside these ranges and needn't reach their ends.
Inputs may be any that keep to these rules, and one draw needn't show every extreme that they name: tile_cols[r, t] lies between max(0, (r // 2 - 1) * 2) and min(16, (r // 2 + 2) * 2) - 1: a block of the row block's own partition or of the partition on either side; a column block may appear several times in a row. `adj_tiles`: each entry is zero or positive; a node's row over its 16 tiles holds about 32 nonzero entries, and its expected sum is one.
All inputs are finite; a program needn't handle non-finite values.
Results may differ from the reference program's by a relative error of at most 0.00085.
Values sent between devices are 32-bit elements; how exact they have to be, the bound alone decides.
A program may use at most 128 MiB of HBM per device.

```python
import math
import jax
import jax.numpy as jnp
from jax import lax

HALF = 256
WIDTH = 512
BLOCK = 128
TILES = 16
LAY_DEV = 2
ROWB_DEV = 2
NBLK = 16
NODES = 2048
LAYERS = 8
N_SEGMENT = 4
N_DOM = 8


def draw_tile_cols(key, part):
    row_index = jnp.arange(NBLK, dtype=jnp.int32)
    owner = row_index // ROWB_DEV
    lowest = jnp.maximum(owner * ROWB_DEV - ROWB_DEV, 0)
    highest = jnp.minimum(owner * ROWB_DEV + 2 * ROWB_DEV, NBLK)
    picks = jax.random.randint(key, (NBLK, TILES), 0, 1 << 20, dtype=jnp.int32)
    return (lowest[:, None] + picks % (highest - lowest)[:, None]).astype(jnp.int32)


def draw_adj_tiles(key, part):
    row_len = TILES * BLOCK
    kept = min(row_len, 32)
    chance = kept / row_len
    key_mask = jax.random.fold_in(key, 7101)
    key_value = jax.random.fold_in(key, 7202)
    shape = (NBLK, TILES, BLOCK, BLOCK)
    mask = (jax.random.uniform(key_mask, shape, jnp.float32) < chance).astype(jnp.float32)
    values = jax.random.uniform(key_value, shape, jnp.float32, 0.5, 1.5)
    return (mask * values / kept).astype(jnp.float32)


def level_of(stream_key, extent, shards, low, largest):
    factor_of, own = 1.0, jax.random.fold_in(stream_key, 6)
    for position, parts in shards:
        draws = jnp.exp(jax.random.uniform(jax.random.fold_in(own, position), (parts,), jnp.float32, low / len(shards), largest / len(shards)))
        factor_of = factor_of * jnp.repeat(draws, extent[position] // parts).reshape([-1 if axis == position else 1 for axis in range(len(extent))])
    return factor_of


def bell_draw(own_key, shape, width, limit, pieces=(), held_as=jnp.bfloat16):
    array = jax.random.normal(own_key, shape, jnp.float32) * width
    if len(pieces) > 0:
        array = level_of(own_key, shape, pieces, -0.22, 0.18) * array
    return jnp.clip(array, min=-limit, max=limit).astype(held_as)


def setup_inputs(seed: int = 0) -> dict:
    keys = jax.random.split(jax.random.key(seed), 13)
    forward_held = bell_draw(keys[0], (N_SEGMENT, NODES, WIDTH), 1.0, 6.0, ((0, 4), (1, 8)), jnp.float32)
    forward_new = bell_draw(keys[1], (NODES, WIDTH), 1.0, 6.0, ((0, 8),), jnp.float32)
    back_outputs = bell_draw(keys[2], (N_SEGMENT, NODES, WIDTH), 1.0, 6.0, ((0, 4), (1, 8)), jnp.float32)
    back_cotangents = bell_draw(keys[3], (N_SEGMENT, NODES, WIDTH), 1.0, 6.0, ((0, 4), (1, 8)), jnp.float32)
    back_new_outputs = bell_draw(keys[4], (NODES, WIDTH), 1.0, 6.0, ((0, 8),), jnp.float32)
    back_new_cotangents = bell_draw(keys[5], (NODES, WIDTH), 1.0, 6.0, ((0, 8),), jnp.float32)
    adj_tiles = draw_adj_tiles(jax.random.fold_in(keys[12], 71), 0)
    tile_cols = draw_tile_cols(jax.random.fold_in(keys[12], 71), 0)
    weight_first = bell_draw(keys[8], (LAYERS, HALF, HALF), HALF ** -0.5, 0.375, ((0, 4),), jnp.float32)
    weight_second = bell_draw(keys[9], (LAYERS, HALF, HALF), HALF ** -0.5, 0.375, ((0, 4),), jnp.float32)
    gain_first = jnp.clip(1.0 + 0.18 * jax.random.normal(keys[10], (LAYERS, HALF), jnp.float32), 0.1, 1.9)
    gain_second = jnp.clip(1.0 + 0.18 * jax.random.normal(keys[11], (LAYERS, HALF), jnp.float32), 0.1, 1.9)
    return {"forward_held": forward_held, "forward_new": forward_new, "back_outputs": back_outputs, "back_cotangents": back_cotangents, "back_new_outputs": back_new_outputs, "back_new_cotangents": back_new_cotangents, "adj_tiles": adj_tiles, "tile_cols": tile_cols, "weight_first": weight_first, "weight_second": weight_second, "gain_first": gain_first, "gain_second": gain_second}


PRECISE = lax.Precision.HIGHEST

def prepare(node_rows, gain_vec, weight):
    row_mean = lax.optimization_barrier(jnp.mean(node_rows, axis=1, keepdims=True))
    centred = node_rows - row_mean
    spread = lax.optimization_barrier(jnp.mean(centred * centred, axis=1, keepdims=True))
    normed = centred * lax.rsqrt(spread + 1e-05) * gain_vec
    return jnp.dot(jax.nn.relu(normed), weight, precision=PRECISE)

def window_matrix(adj_tiles, tile_cols, first_block):
    row_blocks = adj_tiles.shape[0]
    block_size = adj_tiles.shape[2]
    places = jnp.arange(3 * row_blocks, dtype=jnp.int32)
    onehot = (tile_cols[:, :, None] - first_block == places[None, None, :]).astype(jnp.float32)
    banded = jnp.einsum('rtw,rtij->riwj', onehot, adj_tiles, precision=PRECISE)
    return banded.reshape(row_blocks * block_size, 3 * row_blocks * block_size)

def reference(forward_held, forward_new, back_outputs, back_cotangents, back_new_outputs, back_new_cotangents, adj_tiles, tile_cols, weight_first, weight_second, gain_first, gain_second):
    shard_rows = ROWB_DEV * BLOCK
    tiles_split = adj_tiles.reshape(N_DOM, ROWB_DEV, TILES, BLOCK, BLOCK)
    cols_split = tile_cols.reshape(N_DOM, ROWB_DEV, TILES).astype(jnp.int32)
    firsts = ((jnp.arange(N_DOM, dtype=jnp.int32) - 1) * ROWB_DEV).astype(jnp.int32)
    band_rows = jax.vmap(window_matrix)(tiles_split, cols_split, firsts)
    zeros_one = jnp.zeros((1, shard_rows, HALF), jnp.float32)

    def aggregate(values):
        blocks = values.reshape(N_DOM, shard_rows, HALF)
        padded = jnp.concatenate([zeros_one, blocks, zeros_one], axis=0)
        windows = jnp.concatenate([padded[:-2], padded[1:-1], padded[2:]], axis=1)
        return jnp.einsum('dnm,dmf->dnf', band_rows, windows, precision=PRECISE).reshape(NODES, HALF)

    def transpose_aggregate(values):
        blocks = values.reshape(N_DOM, shard_rows, HALF)
        contrib = jnp.einsum('dnm,dnf->dmf', band_rows, blocks, precision=PRECISE)
        upper = contrib[:, :shard_rows]
        middle = contrib[:, shard_rows:2 * shard_rows]
        lower = contrib[:, 2 * shard_rows:]
        total = middle + jnp.concatenate([upper[1:], zeros_one], axis=0) + jnp.concatenate([zeros_one, lower[:-1]], axis=0)
        return total.reshape(NODES, HALF)

    def forward_section(section, activations):
        for depth_idx in range(LAY_DEV):
            layer_idx = section * LAY_DEV + depth_idx
            first_half = activations[:, :HALF]
            second_half = activations[:, HALF:]
            first_half = first_half + aggregate(prepare(second_half, gain_first[layer_idx], weight_first[layer_idx]))
            second_half = second_half + aggregate(prepare(first_half, gain_second[layer_idx], weight_second[layer_idx]))
            activations = jnp.concatenate([first_half, second_half], axis=1)
        return activations
    grads_wf = [jnp.zeros((HALF, HALF), jnp.float32) for layer_idx in range(LAYERS)]
    grads_ws = [jnp.zeros((HALF, HALF), jnp.float32) for layer_idx in range(LAYERS)]
    grads_gf = [jnp.zeros((HALF,), jnp.float32) for layer_idx in range(LAYERS)]
    grads_gs = [jnp.zeros((HALF,), jnp.float32) for layer_idx in range(LAYERS)]

    def backward_section(section, outputs, cotangents):
        for depth_idx in reversed(range(LAY_DEV)):
            layer_idx = section * LAY_DEV + depth_idx
            upper_out = outputs[:, :HALF]
            lower_out = outputs[:, HALF:]
            upper_cot = cotangents[:, :HALF]
            lower_cot = cotangents[:, HALF:]
            mixed_second, pull_second = jax.vjp(prepare, upper_out, gain_second[layer_idx], weight_second[layer_idx])
            lower_in = lower_out - aggregate(mixed_second)
            extra_upper, dgain_second, dweight_second = pull_second(transpose_aggregate(lower_cot))
            carried = upper_cot + extra_upper
            mixed_first, pull_first = jax.vjp(prepare, lower_in, gain_first[layer_idx], weight_first[layer_idx])
            upper_in = upper_out - aggregate(mixed_first)
            extra_lower, dgain_first, dweight_first = pull_first(transpose_aggregate(carried))
            outputs = jnp.concatenate([upper_in, lower_in], axis=1)
            cotangents = jnp.concatenate([carried, lower_cot + extra_lower], axis=1)
            grads_wf[layer_idx] = grads_wf[layer_idx] + dweight_first
            grads_ws[layer_idx] = grads_ws[layer_idx] + dweight_second
            grads_gf[layer_idx] = grads_gf[layer_idx] + dgain_first
            grads_gs[layer_idx] = grads_gs[layer_idx] + dgain_second
        return (outputs, cotangents)
    forward_one = [forward_section(section, forward_held[section]) for section in range(N_SEGMENT)]
    entries = [forward_new] + forward_one[:-1]
    forward_two = [forward_section(section, entries[section]) for section in range(N_SEGMENT)]
    results_one = [backward_section(section, back_outputs[section], back_cotangents[section]) for section in range(N_SEGMENT)]
    results_two = []
    for section in range(N_SEGMENT):
        if section == N_SEGMENT - 1:
            results_two.append(backward_section(section, back_new_outputs, back_new_cotangents))
        else:
            results_two.append(backward_section(section, results_one[section + 1][0], results_one[section + 1][1]))
    scale_factor = 1.0 / math.sqrt(2.0 * NODES)
    return (jnp.stack(forward_one), jnp.stack(forward_two), jnp.stack([pair_item[0] for pair_item in results_one]), jnp.stack([pair_item[1] for pair_item in results_one]), jnp.stack([pair_item[0] for pair_item in results_two]), jnp.stack([pair_item[1] for pair_item in results_two]), jnp.stack(grads_wf) * scale_factor, jnp.stack(grads_ws) * scale_factor, jnp.stack(grads_gf) * scale_factor, jnp.stack(grads_gs) * scale_factor)
```

```python
import functools
import math

import jax
import jax.numpy as jnp
from jax import lax
from jax.experimental import pallas as pl
from jax.experimental.pallas import tpu as pltpu
from jax.sharding import PartitionSpec as P

MESH = pl.DeviceIdType.MESH
F32 = jnp.float32
BF16 = jnp.bfloat16


def split(value):
    high = value.astype(BF16)
    return high, (value - high.astype(F32)).astype(BF16)


def split6(value):
    high = value.astype(BF16)
    rest = value - high.astype(F32)
    mid = rest.astype(BF16)
    return high, mid, (rest - mid.astype(F32)).astype(BF16)


def dot(a, b, dims=((1,), (0,))):
    return lax.dot_general(a, b, (dims, ((), ())), preferred_element_type=F32)


def dot3(a, b, dims=((1,), (0,))):
    (ah, al), (bh, bl) = a, b
    return dot(ah, bh, dims) + (dot(ah, bl, dims) + dot(al, bh, dims))


def dot6(a, b):
    (ah, am, al), (bh, bm, bl) = a, b
    small = dot(ah, bl) + dot(al, bh) + dot(am, bm)
    return dot(ah, bh) + (dot(ah, bm) + dot(am, bh) + small)


def kernel(
    doms,
    segs,
    cols,
    fwd_in,
    fwd_new,
    out_in,
    cot_in,
    out_new,
    cot_new,
    tiles,
    wf,
    ws,
    gf,
    gs,
    fwd_one,
    fwd_two,
    in_one,
    ct_one,
    in_two,
    ct_two,
    gwf,
    gws,
    ggf,
    ggs,
    band_h,
    band_l,
    band_x,
    bt_h,
    bt_l,
    w_h,
    w_l,
    w_x,
    st,
    ext,
    ks,
    kr,
    km,
    xh,
    rs,
    hold,
    land,
    grad,
    gland,
    gout,
    send_sem,
    recv_sem,
    hs_sem,
    hr_sem,
    gs_sem,
    gr_sem,
):
    dom = lax.axis_index("dom")
    seg = lax.axis_index("segment")
    S = fwd_new.shape[0]
    H = fwd_new.shape[1] // 2
    L = wf.shape[0]
    rounds = 2 * L
    bits = doms.bit_length() - 1
    has_left, has_right = dom > 0, dom < doms - 1
    has_prev, has_next = seg > 0, seg < segs - 1

    def partner(s):
        bit = (dom // (1 << s)) % 2
        return bit, dom + (1 << s) * (1 - 2 * bit)

    barrier = pltpu.get_barrier_semaphore()

    def greet(where):
        pl.semaphore_signal(barrier, inc=1, device_id=where, device_id_type=MESH)

    for cond, where in (
        (has_left, {"dom": dom - 1}),
        (has_right, {"dom": dom + 1}),
        (has_prev, {"segment": seg - 1}),
        (has_next, {"segment": seg + 1}),
    ):
        pl.when(cond)(functools.partial(greet, where))
    for s in range(bits):
        greet({"dom": partner(s)[1]})

    R, T, B = tiles.shape[0], tiles.shape[1], tiles.shape[2]
    first = (dom - 1) * R
    for r in range(R):
        for w in range(3 * R):
            total = jnp.zeros((B, B), F32)
            for t in range(T):
                total += jnp.where(cols[r, t] == first + w, 1.0, 0.0) * tiles[r, t]
            hi, lo, rest = split6(total)
            band_x[r * B : (r + 1) * B, w * B : (w + 1) * B] = rest
            band_h[r * B : (r + 1) * B, w * B : (w + 1) * B] = hi
            band_l[r * B : (r + 1) * B, w * B : (w + 1) * B] = lo
            hi, lo = split(total.T)
            bt_h[w * B : (w + 1) * B, r * B : (r + 1) * B] = hi
            bt_l[w * B : (w + 1) * B, r * B : (r + 1) * B] = lo
    for j in range(L):
        for k, ref in enumerate((wf, ws)):
            w_h[2 * j + k], w_l[2 * j + k], w_x[2 * j + k] = split6(ref[j])
    grad[...] = jnp.zeros_like(grad)
    zero = jnp.zeros((S, H), F32)

    @pl.when(jnp.logical_not(has_left))
    def _():
        for par in range(2):
            ext[0, par, :S] = zero
            ext[1, par, :S] = zero
            kr[par, :S] = zero

    @pl.when(jnp.logical_not(has_right))
    def _():
        for par in range(2):
            ext[0, par, 2 * S :] = zero
            ext[1, par, 2 * S :] = zero
            kr[par, S:] = zero

    expected = (
        bits
        + has_left.astype(jnp.int32)
        + has_right.astype(jnp.int32)
        + has_prev.astype(jnp.int32)
        + has_next.astype(jnp.int32)
    )
    pl.semaphore_wait(barrier, expected)

    def to_left(chain, par):
        if chain == 2:
            src, dst = ks.at[par, :S], kr.at[par, S:]
        else:
            src, dst = ext.at[chain, par, S : 2 * S], ext.at[chain, par, 2 * S :]
        return pltpu.make_async_remote_copy(
            src, dst, send_sem.at[chain, par, 0], recv_sem.at[chain, par, 0],
            device_id={"dom": dom - 1}, device_id_type=MESH,
        )

    def to_right(chain, par):
        if chain == 2:
            src, dst = ks.at[par, S:], kr.at[par, :S]
        else:
            src, dst = ext.at[chain, par, S : 2 * S], ext.at[chain, par, :S]
        return pltpu.make_async_remote_copy(
            src, dst, send_sem.at[chain, par, 1], recv_sem.at[chain, par, 1],
            device_id={"dom": dom + 1}, device_id_type=MESH,
        )

    def start(chain, par):
        @pl.when(has_left)
        def _():
            to_left(chain, par).start()

        @pl.when(has_right)
        def _():
            to_right(chain, par).start()

    def finish(chain, par):
        @pl.when(has_left)
        def _():
            to_left(chain, par).wait_send()
            to_right(chain, par).wait_recv()

        @pl.when(has_right)
        def _():
            to_right(chain, par).wait_send()
            to_left(chain, par).wait_recv()

    def normed(value):
        centred = value - jnp.mean(value, axis=1, keepdims=True)
        scale = lax.rsqrt(jnp.mean(centred * centred, axis=1, keepdims=True) + 1e-05)
        return centred * scale, scale

    def weight(index):
        return w_h[index], w_l[index]

    def gain(index):
        return (gf, gs)[index % 2][index // 2 : index // 2 + 1, :]

    def emit_forward(r):
        par = r % 2
        xhat, _ = normed(st[1 - par])
        ext[0, par, S : 2 * S] = dot3(split(jnp.maximum(xhat * gain(r), 0.0)), weight(r))
        start(0, par)

    def emit_inverse(r):
        par, index = r % 2, rounds - 1 - r
        xhat, scale = normed(st[2 + par])
        xh[par] = xhat
        rs[par] = scale
        ext[1, par, S : 2 * S] = dot6(
            split6(jnp.maximum(xhat * gain(index), 0.0)), weight(index) + (w_x[index],)
        )
        start(1, par)

    def emit_cotan(r):
        par = r % 2
        value = split(st[5 - par])
        for place in range(2):
            lo, hi = 2 * place * S, (2 * place + 1) * S
            ks[par, place * S : (place + 1) * S] = dot3((bt_h[lo:hi], bt_l[lo:hi]), value)
        start(2, par)
        km[...] = dot3((bt_h[S : 2 * S], bt_l[S : 2 * S]), value)


    def end_forward(r):
        par = r % 2
        finish(0, par)
        st[par] += dot3((band_h[...], band_l[...]), split(ext[0, par]))

    def end_inverse(r):
        par = r % 2
        finish(1, par)
        st[3 - par] -= dot6((band_h[...], band_l[...], band_x[...]), split6(ext[1, par]))

    def end_cotan(r):
        par, index = r % 2, rounds - 1 - r
        finish(2, par)
        total = km[...] + (kr[par, :S] + kr[par, S:])
        parts = split(total)
        xhat = xh[par]
        vec = gain(index)
        pre = xhat * vec
        back = dot3(parts, weight(index), ((1,), (1,)))
        back = jnp.where(pre > 0.0, back, 0.0)
        row = rounds * H + index
        grad[row : row + 1, :] += jnp.sum(back * xhat, axis=0, keepdims=True)
        back = back * vec
        inner = jnp.mean(back * xhat, axis=1, keepdims=True)
        st[4 + par] += rs[par] * (back - jnp.mean(back, axis=1, keepdims=True) - xhat * inner)
        rows = jnp.maximum(pre, 0.0).T
        grad[index * H : (index + 1) * H, :] += dot3(split(rows), parts)

    outs = ((fwd_one, fwd_two), (in_one, in_two), (ct_one, ct_two))

    def hand(chain, half):
        ahead = 1 if chain == 0 else -1
        k = 2 * chain + half
        return pltpu.make_async_remote_copy(
            hold.at[k], land.at[k],
            hs_sem.at[k], hr_sem.at[k],
            device_id={"segment": seg + ahead}, device_id_type=MESH,
        )

    def can_send(chain):
        return has_next if chain == 0 else has_prev

    def can_take(chain):
        return has_prev if chain == 0 else has_next

    def store(slot, chain, half):
        @pl.when(slot == 0)
        def _():
            outs[chain][0][0, :, half * H : (half + 1) * H] = st[2 * chain + half]
            hold[2 * chain + half] = st[2 * chain + half]
            pl.when(can_send(chain))(lambda: hand(chain, half).start())

        @pl.when(slot == 1)
        def _():
            outs[chain][1][0, :, half * H : (half + 1) * H] = st[2 * chain + half]

    olds, news = (fwd_in, out_in, cot_in), (fwd_new, out_new, cot_new)

    def load(slot, chain):
        @pl.when(slot == 0)
        def _():
            for half in range(2):
                st[2 * chain + half] = olds[chain][0, :, half * H : (half + 1) * H]

        @pl.when(jnp.logical_and(slot == 1, jnp.logical_not(can_take(chain))))
        def _():
            for half in range(2):
                st[2 * chain + half] = news[chain][:, half * H : (half + 1) * H]

        @pl.when(jnp.logical_and(slot == 1, can_take(chain)))
        def _():
            for half in range(2):
                hand(chain, half).wait_recv()
                st[2 * chain + half] = land[2 * chain + half]

    emits = (emit_forward, emit_inverse, emit_cotan)
    ends = (end_forward, end_inverse, end_cotan)

    def run_slot(slot, carry):
        for chain in range(3):
            load(slot, chain)
            emits[chain](0)
        for r in range(rounds):
            for chain in range(3):
                ends[chain](r)
                if r + 1 < rounds:
                    emits[chain](r + 1)
                if r >= rounds - 2:
                    store(slot, chain, r % 2 if chain != 1 else 1 - r % 2)
        return carry

    lax.fori_loop(0, 2, run_slot, 0)

    rows = grad.shape[0]
    offset, size, used = 0, rows, 0
    steps = []
    for s in range(bits):
        bit, other = partner(s)
        size = size // 2
        keep = pl.multiple_of(offset + bit * size, 8)
        give = pl.multiple_of(offset + (1 - bit) * size, 8)
        copy = pltpu.make_async_remote_copy(
            grad.at[pl.ds(give, size)], gland.at[used : used + size],
            gs_sem.at[0, s], gr_sem.at[0, s],
            device_id={"dom": other}, device_id_type=MESH,
        )
        copy.start()
        copy.wait()
        grad[pl.ds(keep, size), :] += gland[used : used + size, :]
        steps.append((s, other, keep, size))
        used, offset = used + size, keep
    gout[pl.ds(offset, size), :] = grad[pl.ds(offset, size), :]
    for s, other, keep, size in reversed(steps):
        copy = pltpu.make_async_remote_copy(
            gout.at[pl.ds(keep, size)], gout.at[pl.ds(keep, size)],
            gs_sem.at[1, s], gr_sem.at[1, s],
            device_id={"dom": other}, device_id_type=MESH,
        )
        copy.start()
        copy.wait()
    scale = 1.0 / math.sqrt(2.0 * S * doms)
    for j in range(L):
        for k, (wref, gref) in enumerate(((gwf, ggf), (gws, ggs))):
            index = 2 * j + k
            wref[j] = gout[index * H : (index + 1) * H, :] * scale
            row = rounds * H + index
            gref[j : j + 1, :] = gout[row : row + 1, :] * scale
    for chain in range(3):
        for half in range(2):
            pl.when(can_send(chain))(lambda c=chain, h=half: hand(c, h).wait_send())


def per_device(doms, segs, *args):
    (held, new, bo, bc, bno, bnc, tiles, cols, wf, ws, gf, gs) = args
    S, W = new.shape
    H, L = W // 2, wf.shape[0]
    bits = doms.bit_length() - 1
    rows = 2 * L * H + 8 * doms
    state = jax.ShapeDtypeStruct((1, S, W), F32)
    vmem = pl.BlockSpec(memory_space=pltpu.VMEM)
    results = pl.pallas_call(
        functools.partial(kernel, doms, segs),
        out_shape=[state] * 6
        + [jax.ShapeDtypeStruct((L, H, H), F32)] * 2
        + [jax.ShapeDtypeStruct((L, H), F32)] * 2,
        in_specs=[pl.BlockSpec(memory_space=pltpu.SMEM)] + [vmem] * 11,
        out_specs=[vmem] * 10,
        scratch_shapes=[
            pltpu.VMEM((S, 3 * S), BF16),
            pltpu.VMEM((S, 3 * S), BF16),
            pltpu.VMEM((S, 3 * S), BF16),
            pltpu.VMEM((3 * S, S), BF16),
            pltpu.VMEM((3 * S, S), BF16),
            pltpu.VMEM((2 * L, H, H), BF16),
            pltpu.VMEM((2 * L, H, H), BF16),
            pltpu.VMEM((2 * L, H, H), BF16),
            pltpu.VMEM((6, S, H), F32),
            pltpu.VMEM((2, 2, 3 * S, H), F32),
            pltpu.VMEM((2, 2 * S, H), F32),
            pltpu.VMEM((2, 2 * S, H), F32),
            pltpu.VMEM((S, H), F32),
            pltpu.VMEM((2, S, H), F32),
            pltpu.VMEM((2, S, 1), F32),
            pltpu.VMEM((6, S, H), F32),
            pltpu.VMEM((6, S, H), F32),
            pltpu.VMEM((rows, H), F32),
            pltpu.VMEM((rows, H), F32),
            pltpu.VMEM((rows, H), F32),
            pltpu.SemaphoreType.DMA((3, 2, 2)),
            pltpu.SemaphoreType.DMA((3, 2, 2)),
            pltpu.SemaphoreType.DMA((6,)),
            pltpu.SemaphoreType.DMA((6,)),
            pltpu.SemaphoreType.DMA((2, bits)),
            pltpu.SemaphoreType.DMA((2, bits)),
        ],
        compiler_params=pltpu.CompilerParams(
            collective_id=0, has_side_effects=True, vmem_limit_bytes=60 * 1024 * 1024
        ),
    )(cols, held, new, bo, bc, bno, bnc, tiles, wf, ws, gf, gs)
    return tuple(results)


def solution(mesh):
    row = P("segment", "dom", None)
    flat = P("dom", None)
    cube = P("segment", None, None)
    vec = P("segment", None)
    return jax.shard_map(
        functools.partial(per_device, mesh.shape["dom"], mesh.shape["segment"]),
        mesh=mesh,
        in_specs=(
            row, flat, row, row, flat, flat,
            P("dom", None, None, None), flat, cube, cube, vec, vec,
        ),
        out_specs=(row,) * 6 + (cube, cube, vec, vec),
        check_vma=False,
    )
```

```python
import functools
import math

import jax
import jax.numpy as jnp
from jax import lax
from jax.experimental import pallas as pl
from jax.experimental.pallas import tpu as pltpu
from jax.sharding import PartitionSpec as P

MESH = pl.DeviceIdType.MESH
F32 = jnp.float32
BF16 = jnp.bfloat16


def split(value):
    high = value.astype(BF16)
    return high, (value - high.astype(F32)).astype(BF16)


def split6(value):
    high = value.astype(BF16)
    rest = value - high.astype(F32)
    mid = rest.astype(BF16)
    return high, mid, (rest - mid.astype(F32)).astype(BF16)


def dot(a, b, dims=((1,), (0,))):
    return lax.dot_general(a, b, (dims, ((), ())), preferred_element_type=F32)


def dot3(a, b, dims=((1,), (0,))):
    (ah, al), (bh, bl) = a, b
    return dot(ah, bh, dims) + (dot(ah, bl, dims) + dot(al, bh, dims))


def dot6(a, b):
    (ah, am, al), (bh, bm, bl) = a, b
    small = dot(ah, bl) + dot(al, bh) + dot(am, bm)
    return dot(ah, bh) + (dot(ah, bm) + dot(am, bh) + small)


def kernel(
    doms,
    segs,
    cols,
    fwd_in,
    fwd_new,
    out_in,
    cot_in,
    out_new,
    cot_new,
    tiles,
    wf,
    ws,
    gf,
    gs,
    fwd_one,
    fwd_two,
    in_one,
    ct_one,
    in_two,
    ct_two,
    gwf,
    gws,
    ggf,
    ggs,
    band_h,
    band_l,
    band_x,
    bt_h,
    bt_l,
    w_h,
    w_l,
    w_x,
    st,
    ext,
    ks,
    kr,
    km,
    xh,
    rs,
    hold,
    land,
    grad,
    gland,
    gout,
    send_sem,
    recv_sem,
    hs_sem,
    hr_sem,
    gs_sem,
    gr_sem,
):
    dom = lax.axis_index("dom")
    seg = lax.axis_index("segment")
    S = fwd_new.shape[0]
    H = fwd_new.shape[1] // 2
    L = wf.shape[0]
    rounds = 2 * L
    bits = doms.bit_length() - 1
    has_left, has_right = dom > 0, dom < doms - 1
    has_prev, has_next = seg > 0, seg < segs - 1

    def partner(s):
        bit = (dom // (1 << s)) % 2
        return bit, dom + (1 << s) * (1 - 2 * bit)

    barrier = pltpu.get_barrier_semaphore()

    def greet(where):
        pl.semaphore_signal(barrier, inc=1, device_id=where, device_id_type=MESH)

    for cond, where in (
        (has_left, {"dom": dom - 1}),
        (has_right, {"dom": dom + 1}),
        (has_prev, {"segment": seg - 1}),
        (has_next, {"segment": seg + 1}),
    ):
        pl.when(cond)(functools.partial(greet, where))
    for s in range(bits):
        greet({"dom": partner(s)[1]})

    R, T, B = tiles.shape[0], tiles.shape[1], tiles.shape[2]
    first = (dom - 1) * R
    for r in range(R):
        for w in range(3 * R):
            total = jnp.zeros((B, B), F32)
            for t in range(T):
                total += jnp.where(cols[r, t] == first + w, 1.0, 0.0) * tiles[r, t]
            hi, lo, rest = split6(total)
            band_x[r * B : (r + 1) * B, w * B : (w + 1) * B] = rest
            band_h[r * B : (r + 1) * B, w * B : (w + 1) * B] = hi
            band_l[r * B : (r + 1) * B, w * B : (w + 1) * B] = lo
            hi, lo = split(total.T)
            bt_h[w * B : (w + 1) * B, r * B : (r + 1) * B] = hi
            bt_l[w * B : (w + 1) * B, r * B : (r + 1) * B] = lo
    for j in range(L):
        for k, ref in enumerate((wf, ws)):
            w_h[2 * j + k], w_l[2 * j + k], w_x[2 * j + k] = split6(ref[j])
    grad[...] = jnp.zeros_like(grad)
    zero = jnp.zeros((S, H), F32)

    @pl.when(jnp.logical_not(has_left))
    def _():
        for par in range(2):
            ext[0, par, :S] = zero
            ext[1, par, :S] = zero
            kr[par, :S] = zero

    @pl.when(jnp.logical_not(has_right))
    def _():
        for par in range(2):
            ext[0, par, 2 * S :] = zero
            ext[1, par, 2 * S :] = zero
            kr[par, S:] = zero

    expected = (
        bits
        + has_left.astype(jnp.int32)
        + has_right.astype(jnp.int32)
        + has_prev.astype(jnp.int32)
        + has_next.astype(jnp.int32)
    )
    pl.semaphore_wait(barrier, expected)

    def to_left(chain, par):
        if chain == 2:
            src, dst = ks.at[par, :S], kr.at[par, S:]
        else:
            src, dst = ext.at[chain, par, S : 2 * S], ext.at[chain, par, 2 * S :]
        return pltpu.make_async_remote_copy(
            src, dst, send_sem.at[chain, par, 0], recv_sem.at[chain, par, 0],
            device_id={"dom": dom - 1}, device_id_type=MESH,
        )

    def to_right(chain, par):
        if chain == 2:
            src, dst = ks.at[par, S:], kr.at[par, :S]
        else:
            src, dst = ext.at[chain, par, S : 2 * S], ext.at[chain, par, :S]
        return pltpu.make_async_remote_copy(
            src, dst, send_sem.at[chain, par, 1], recv_sem.at[chain, par, 1],
            device_id={"dom": dom + 1}, device_id_type=MESH,
        )

    def start(chain, par):
        @pl.when(has_left)
        def _():
            to_left(chain, par).start()

        @pl.when(has_right)
        def _():
            to_right(chain, par).start()

    def finish(chain, par):
        @pl.when(has_left)
        def _():
            to_left(chain, par).wait_send()
            to_right(chain, par).wait_recv()

        @pl.when(has_right)
        def _():
            to_right(chain, par).wait_send()
            to_left(chain, par).wait_recv()

    def normed(value):
        centred = value - jnp.mean(value, axis=1, keepdims=True)
        scale = lax.rsqrt(jnp.mean(centred * centred, axis=1, keepdims=True) + 1e-05)
        return centred * scale, scale

    def weight(index):
        return w_h[index], w_l[index]

    def gain(index):
        return (gf, gs)[index % 2][index // 2 : index // 2 + 1, :]

    def emit_forward(r):
        par = r % 2
        xhat, _ = normed(st[1 - par])
        ext[0, par, S : 2 * S] = dot3(split(jnp.maximum(xhat * gain(r), 0.0)), weight(r))
        start(0, par)

    def emit_inverse(r):
        par, index = r % 2, rounds - 1 - r
        xhat, scale = normed(st[2 + par])
        xh[par] = xhat
        rs[par] = scale
        ext[1, par, S : 2 * S] = dot6(
            split6(jnp.maximum(xhat * gain(index), 0.0)), weight(index) + (w_x[index],)
        )
        start(1, par)

    def emit_cotan(r):
        par = r % 2
        value = split(st[5 - par])
        for place in range(2):
            lo, hi = 2 * place * S, (2 * place + 1) * S
            ks[par, place * S : (place + 1) * S] = dot3((bt_h[lo:hi], bt_l[lo:hi]), value)
        start(2, par)
        km[...] = dot3((bt_h[S : 2 * S], bt_l[S : 2 * S]), value)


    def end_forward(r):
        par = r % 2
        finish(0, par)
        st[par] += dot3((band_h[...], band_l[...]), split(ext[0, par]))

    def end_inverse(r):
        par = r % 2
        finish(1, par)
        st[3 - par] -= dot6((band_h[...], band_l[...], band_x[...]), split6(ext[1, par]))

    def end_cotan(r):
        par, index = r % 2, rounds - 1 - r
        finish(2, par)
        total = km[...] + (kr[par, :S] + kr[par, S:])
        parts = split(total)
        xhat = xh[par]
        vec = gain(index)
        pre = xhat * vec
        back = dot3(parts, weight(index), ((1,), (1,)))
        back = jnp.where(pre > 0.0, back, 0.0)
        row = rounds * H + index
        grad[row : row + 1, :] += jnp.sum(back * xhat, axis=0, keepdims=True)
        back = back * vec
        inner = jnp.mean(back * xhat, axis=1, keepdims=True)
        st[4 + par] += rs[par] * (back - jnp.mean(back, axis=1, keepdims=True) - xhat * inner)
        rows = jnp.maximum(pre, 0.0).T
        base = (rounds - 1 - index) * H
        grad[base : base + H, :] += dot3(split(rows), parts)

    outs = ((fwd_one, fwd_two), (in_one, in_two), (ct_one, ct_two))

    def hand(chain, half):
        ahead = 1 if chain == 0 else -1
        k = 2 * chain + half
        return pltpu.make_async_remote_copy(
            hold.at[k], land.at[k],
            hs_sem.at[k], hr_sem.at[k],
            device_id={"segment": seg + ahead}, device_id_type=MESH,
        )

    def can_send(chain):
        return has_next if chain == 0 else has_prev

    def can_take(chain):
        return has_prev if chain == 0 else has_next

    def store(slot, chain, half):
        @pl.when(slot == 0)
        def _():
            outs[chain][0][0, :, half * H : (half + 1) * H] = st[2 * chain + half]
            hold[2 * chain + half] = st[2 * chain + half]
            pl.when(can_send(chain))(lambda: hand(chain, half).start())

        @pl.when(slot == 1)
        def _():
            outs[chain][1][0, :, half * H : (half + 1) * H] = st[2 * chain + half]

    olds, news = (fwd_in, out_in, cot_in), (fwd_new, out_new, cot_new)

    def load(slot, chain):
        @pl.when(slot == 0)
        def _():
            for half in range(2):
                st[2 * chain + half] = olds[chain][0, :, half * H : (half + 1) * H]

        @pl.when(jnp.logical_and(slot == 1, jnp.logical_not(can_take(chain))))
        def _():
            for half in range(2):
                st[2 * chain + half] = news[chain][:, half * H : (half + 1) * H]

        @pl.when(jnp.logical_and(slot == 1, can_take(chain)))
        def _():
            for half in range(2):
                hand(chain, half).wait_recv()
                st[2 * chain + half] = land[2 * chain + half]

    plans, landed = [], 0
    for q in range(rounds):
        offset, size = q * H, H if q + 1 < rounds else grad.shape[0] - q * H
        halvings, doublings = [], []
        for s in range(bits):
            bit, other = partner(s)
            give = offset
            if size % 16 == 0:
                size = size // 2
                give = pl.multiple_of(offset + (1 - bit) * size, 8)
                offset = pl.multiple_of(offset + bit * size, 8)
                doublings.insert(0, (other, offset, offset, size, None))
            halvings.append((other, give, offset, size, landed))
            landed += size
        plans.append(halvings + doublings)
    pointer = [0] * rounds

    def piece(q, phase):
        other, give, keep, size, place = plans[q][phase]
        if place is None:
            src, dst = gout.at[pl.ds(give, size)], gout.at[pl.ds(give, size)]
        else:
            src, dst = grad.at[pl.ds(give, size)], gland.at[place : place + size]
        return pltpu.make_async_remote_copy(
            src, dst, gs_sem.at[q, phase], gr_sem.at[q, phase],
            device_id={"dom": other}, device_id_type=MESH,
        )

    def pump(q):
        phase = pointer[q]
        pointer[q] = phase + 1
        if 0 < phase <= len(plans[q]):
            piece(q, phase - 1).wait()
            other, give, keep, size, place = plans[q][phase - 1]
            if place is not None:
                total = grad[pl.ds(keep, size), :] + gland[place : place + size, :]
                if phase == bits:
                    gout[pl.ds(keep, size), :] = total
                else:
                    grad[pl.ds(keep, size), :] = total
        if phase < len(plans[q]):
            piece(q, phase).start()

    emits = (emit_forward, emit_inverse, emit_cotan)
    ends = (end_forward, end_inverse, end_cotan)

    def run_slot(slot, carry):
        pointer[:] = [0] * rounds
        for chain in range(3):
            load(slot, chain)
            emits[chain](0)
        for r in range(rounds):
            for chain in range(3):
                ends[chain](r)
                if r + 1 < rounds:
                    emits[chain](r + 1)
                ready = range(r + 1 if chain == 2 else r)
                if ready:

                    @pl.when(slot == 1)
                    def _():
                        for q in ready:
                            if q + 1 < rounds:
                                pump(q)

                if r >= rounds - 2:
                    store(slot, chain, r % 2 if chain != 1 else 1 - r % 2)
        return carry

    lax.fori_loop(0, 2, run_slot, 0)

    while any(pointer[q] <= len(plans[q]) for q in range(rounds)):
        for q in range(rounds):
            pump(q)
    scale = 1.0 / math.sqrt(2.0 * S * doms)
    for j in range(L):
        for k, (wref, gref) in enumerate(((gwf, ggf), (gws, ggs))):
            index = 2 * j + k
            base = (rounds - 1 - index) * H
            wref[j] = gout[base : base + H, :] * scale
            row = rounds * H + index
            gref[j : j + 1, :] = gout[row : row + 1, :] * scale
    for chain in range(3):
        for half in range(2):
            pl.when(can_send(chain))(lambda c=chain, h=half: hand(c, h).wait_send())


def publish(*refs):
    sems = refs[-1]
    count = len(refs) // 2
    copies = [
        pltpu.make_async_copy(refs[i], refs[count + i], sems.at[i]) for i in range(count)
    ]
    for copy in copies:
        copy.start()
    for copy in copies:
        copy.wait()


def per_device(doms, segs, *args):
    (held, new, bo, bc, bno, bnc, tiles, cols, wf, ws, gf, gs) = args
    S, W = new.shape
    H, L = W // 2, wf.shape[0]
    bits = doms.bit_length() - 1
    rows = 2 * L * H + 8 * doms
    state = jax.ShapeDtypeStruct((1, S, W), F32)
    vmem = pl.BlockSpec(memory_space=pltpu.VMEM)
    results = pl.pallas_call(
        functools.partial(kernel, doms, segs),
        out_shape=[state] * 6
        + [jax.ShapeDtypeStruct((L, H, H), F32)] * 2
        + [jax.ShapeDtypeStruct((L, H), F32)] * 2,
        in_specs=[pl.BlockSpec(memory_space=pltpu.SMEM)] + [vmem] * 11,
        out_specs=[vmem] * 10,
        scratch_shapes=[
            pltpu.VMEM((S, 3 * S), BF16),
            pltpu.VMEM((S, 3 * S), BF16),
            pltpu.VMEM((S, 3 * S), BF16),
            pltpu.VMEM((3 * S, S), BF16),
            pltpu.VMEM((3 * S, S), BF16),
            pltpu.VMEM((2 * L, H, H), BF16),
            pltpu.VMEM((2 * L, H, H), BF16),
            pltpu.VMEM((2 * L, H, H), BF16),
            pltpu.VMEM((6, S, H), F32),
            pltpu.VMEM((2, 2, 3 * S, H), F32),
            pltpu.VMEM((2, 2 * S, H), F32),
            pltpu.VMEM((2, 2 * S, H), F32),
            pltpu.VMEM((S, H), F32),
            pltpu.VMEM((2, S, H), F32),
            pltpu.VMEM((2, S, 1), F32),
            pltpu.VMEM((6, S, H), F32),
            pltpu.VMEM((6, S, H), F32),
            pltpu.VMEM((rows, H), F32),
            pltpu.VMEM((2 * rows, H), F32),
            pltpu.VMEM((rows, H), F32),
            pltpu.SemaphoreType.DMA((3, 2, 2)),
            pltpu.SemaphoreType.DMA((3, 2, 2)),
            pltpu.SemaphoreType.DMA((6,)),
            pltpu.SemaphoreType.DMA((6,)),
            pltpu.SemaphoreType.DMA((2 * L, 2 * bits)),
            pltpu.SemaphoreType.DMA((2 * L, 2 * bits)),
        ],
        compiler_params=pltpu.CompilerParams(
            collective_id=0, has_side_effects=True, vmem_limit_bytes=60 * 1024 * 1024
        ),
    )(cols, held, new, bo, bc, bno, bnc, tiles, wf, ws, gf, gs)
    shapes = [jax.ShapeDtypeStruct(r.shape, r.dtype) for r in results]
    count = len(shapes)
    return tuple(
        pl.pallas_call(
            publish,
            out_shape=shapes,
            in_specs=[vmem] * count,
            out_specs=[pl.BlockSpec(memory_space=pl.ANY)] * count,
            scratch_shapes=[pltpu.SemaphoreType.DMA((count,))],
        )(*results)
    )


def solution(mesh):
    row = P("segment", "dom", None)
    flat = P("dom", None)
    cube = P("segment", None, None)
    vec = P("segment", None)
    return jax.shard_map(
        functools.partial(per_device, mesh.shape["dom"], mesh.shape["segment"]),
        mesh=mesh,
        in_specs=(
            row, flat, row, row, flat, flat,
            P("dom", None, None, None), flat, cube, cube, vec, vec,
        ),
        out_specs=(row,) * 6 + (cube, cube, vec, vec),
        check_vma=False,
    )
```

```python
import functools
import math

import jax
import jax.numpy as jnp
from jax import lax
from jax.experimental import pallas as pl
from jax.experimental.pallas import tpu as pltpu
from jax.sharding import PartitionSpec as P

MESH = pl.DeviceIdType.MESH
F32 = jnp.float32
BF16 = jnp.bfloat16


def split(value):
    high = value.astype(BF16)
    return high, (value - high.astype(F32)).astype(BF16)


def split6(value):
    high = value.astype(BF16)
    rest = value - high.astype(F32)
    mid = rest.astype(BF16)
    return high, mid, (rest - mid.astype(F32)).astype(BF16)


def dot(a, b, dims=((1,), (0,))):
    return lax.dot_general(a, b, (dims, ((), ())), preferred_element_type=F32)


def dot3(a, b, dims=((1,), (0,))):
    (ah, al), (bh, bl) = a, b
    return dot(ah, bh, dims) + (dot(ah, bl, dims) + dot(al, bh, dims))


def dot6(a, b):
    (ah, am, al), (bh, bm, bl) = a, b
    small = dot(ah, bl) + dot(al, bh) + dot(am, bm)
    return dot(ah, bh) + (dot(ah, bm) + dot(am, bh) + small)


def kernel(
    doms,
    segs,
    cols,
    fwd_in,
    fwd_new,
    out_in,
    cot_in,
    out_new,
    cot_new,
    tiles,
    wf,
    ws,
    gf,
    gs,
    fwd_one,
    fwd_two,
    in_one,
    ct_one,
    in_two,
    ct_two,
    gwf,
    gws,
    ggf,
    ggs,
    band_h,
    band_l,
    band_x,
    bt_h,
    bt_l,
    w_h,
    w_l,
    w_x,
    st,
    ext,
    ks,
    kr,
    km,
    xh,
    rs,
    hold,
    land,
    grad,
    gland,
    gout,
    send_sem,
    recv_sem,
    hs_sem,
    hr_sem,
    gs_sem,
    gr_sem,
):
    dom = lax.axis_index("dom")
    seg = lax.axis_index("segment")
    S = fwd_new.shape[0]
    H = fwd_new.shape[1] // 2
    L = wf.shape[0]
    rounds = 2 * L
    bits = doms.bit_length() - 1
    has_left, has_right = dom > 0, dom < doms - 1
    has_prev, has_next = seg > 0, seg < segs - 1

    def partner(s):
        bit = (dom // (1 << s)) % 2
        return bit, dom + (1 << s) * (1 - 2 * bit)

    barrier = pltpu.get_barrier_semaphore()

    def greet(where):
        pl.semaphore_signal(barrier, inc=1, device_id=where, device_id_type=MESH)

    for cond, where in (
        (has_left, {"dom": dom - 1}),
        (has_right, {"dom": dom + 1}),
        (has_prev, {"segment": seg - 1}),
        (has_next, {"segment": seg + 1}),
    ):
        pl.when(cond)(functools.partial(greet, where))
    for s in range(bits):
        greet({"dom": partner(s)[1]})

    R, T, B = tiles.shape[0], tiles.shape[1], tiles.shape[2]
    first = (dom - 1) * R
    for r in range(R):
        for w in range(3 * R):
            total = jnp.zeros((B, B), F32)
            for t in range(T):
                total += jnp.where(cols[r, t] == first + w, 1.0, 0.0) * tiles[r, t]
            hi, lo, rest = split6(total)
            band_x[r * B : (r + 1) * B, w * B : (w + 1) * B] = rest
            band_h[r * B : (r + 1) * B, w * B : (w + 1) * B] = hi
            band_l[r * B : (r + 1) * B, w * B : (w + 1) * B] = lo
            hi, lo = split(total.T)
            bt_h[w * B : (w + 1) * B, r * B : (r + 1) * B] = hi
            bt_l[w * B : (w + 1) * B, r * B : (r + 1) * B] = lo
    for j in range(L):
        for k, ref in enumerate((wf, ws)):
            w_h[2 * j + k], w_l[2 * j + k], w_x[2 * j + k] = split6(ref[j])
    grad[...] = jnp.zeros_like(grad)
    zero = jnp.zeros((S, H), F32)

    @pl.when(jnp.logical_not(has_left))
    def _():
        for par in range(2):
            ext[0, par, :S] = zero
            ext[1, par, :S] = zero
            kr[par, :S] = zero

    @pl.when(jnp.logical_not(has_right))
    def _():
        for par in range(2):
            ext[0, par, 2 * S :] = zero
            ext[1, par, 2 * S :] = zero
            kr[par, S:] = zero

    expected = (
        bits
        + has_left.astype(jnp.int32)
        + has_right.astype(jnp.int32)
        + has_prev.astype(jnp.int32)
        + has_next.astype(jnp.int32)
    )
    pl.semaphore_wait(barrier, expected)

    def to_left(chain, par):
        if chain == 2:
            src, dst = ks.at[par, :S], kr.at[par, S:]
        else:
            src, dst = ext.at[chain, par, S : 2 * S], ext.at[chain, par, 2 * S :]
        return pltpu.make_async_remote_copy(
            src, dst, send_sem.at[chain, par, 0], recv_sem.at[chain, par, 0],
            device_id={"dom": dom - 1}, device_id_type=MESH,
        )

    def to_right(chain, par):
        if chain == 2:
            src, dst = ks.at[par, S:], kr.at[par, :S]
        else:
            src, dst = ext.at[chain, par, S : 2 * S], ext.at[chain, par, :S]
        return pltpu.make_async_remote_copy(
            src, dst, send_sem.at[chain, par, 1], recv_sem.at[chain, par, 1],
            device_id={"dom": dom + 1}, device_id_type=MESH,
        )

    def start(chain, par):
        @pl.when(has_left)
        def _():
            to_left(chain, par).start()

        @pl.when(has_right)
        def _():
            to_right(chain, par).start()

    def finish(chain, par):
        @pl.when(has_left)
        def _():
            to_left(chain, par).wait_send()
            to_right(chain, par).wait_recv()

        @pl.when(has_right)
        def _():
            to_right(chain, par).wait_send()
            to_left(chain, par).wait_recv()

    def normed(value):
        centred = value - jnp.mean(value, axis=1, keepdims=True)
        scale = lax.rsqrt(jnp.mean(centred * centred, axis=1, keepdims=True) + 1e-05)
        return centred * scale, scale

    def weight(index):
        return w_h[index], w_l[index]

    def gain(index):
        return (gf, gs)[index % 2][index // 2 : index // 2 + 1, :]

    def emit_forward(r):
        par = r % 2
        xhat, _ = normed(st[1 - par])
        ext[0, par, S : 2 * S] = dot3(split(jnp.maximum(xhat * gain(r), 0.0)), weight(r))
        start(0, par)

    def emit_inverse(r):
        par, index = r % 2, rounds - 1 - r
        xhat, scale = normed(st[2 + par])
        xh[par] = xhat
        rs[par] = scale
        ext[1, par, S : 2 * S] = dot6(
            split6(jnp.maximum(xhat * gain(index), 0.0)), weight(index) + (w_x[index],)
        )
        start(1, par)

    def emit_cotan(r):
        par = r % 2
        value = split(st[5 - par])
        for place in range(2):
            lo, hi = 2 * place * S, (2 * place + 1) * S
            ks[par, place * S : (place + 1) * S] = dot3((bt_h[lo:hi], bt_l[lo:hi]), value)
        start(2, par)
        km[...] = dot3((bt_h[S : 2 * S], bt_l[S : 2 * S]), value)


    def end_forward(r):
        par = r % 2
        finish(0, par)
        st[par] += dot3((band_h[...], band_l[...]), split(ext[0, par]))

    def end_inverse(r):
        par = r % 2
        finish(1, par)
        st[3 - par] -= dot6((band_h[...], band_l[...], band_x[...]), split6(ext[1, par]))

    def end_cotan(r):
        par, index = r % 2, rounds - 1 - r
        finish(2, par)
        total = km[...] + (kr[par, :S] + kr[par, S:])
        parts = split(total)
        xhat = xh[par]
        vec = gain(index)
        pre = xhat * vec
        back = dot3(parts, weight(index), ((1,), (1,)))
        back = jnp.where(pre > 0.0, back, 0.0)
        row = rounds * H + index
        grad[row : row + 1, :] += jnp.sum(back * xhat, axis=0, keepdims=True)
        back = back * vec
        inner = jnp.mean(back * xhat, axis=1, keepdims=True)
        st[4 + par] += rs[par] * (back - jnp.mean(back, axis=1, keepdims=True) - xhat * inner)
        rows = jnp.maximum(pre, 0.0).T
        base = (rounds - 1 - index) * H
        grad[base : base + H, :] += dot3(split(rows), parts)

    outs = ((fwd_one, fwd_two), (in_one, in_two), (ct_one, ct_two))

    def hand(chain, half):
        ahead = 1 if chain == 0 else -1
        k = 2 * chain + half
        return pltpu.make_async_remote_copy(
            hold.at[k], land.at[k],
            hs_sem.at[k], hr_sem.at[k],
            device_id={"segment": seg + ahead}, device_id_type=MESH,
        )

    def can_send(chain):
        return has_next if chain == 0 else has_prev

    def can_take(chain):
        return has_prev if chain == 0 else has_next

    def store(slot, chain, half):
        @pl.when(slot == 0)
        def _():
            outs[chain][0][0, :, half * H : (half + 1) * H] = st[2 * chain + half]
            hold[2 * chain + half] = st[2 * chain + half]
            pl.when(can_send(chain))(lambda: hand(chain, half).start())

        @pl.when(slot == 1)
        def _():
            outs[chain][1][0, :, half * H : (half + 1) * H] = st[2 * chain + half]

    olds, news = (fwd_in, out_in, cot_in), (fwd_new, out_new, cot_new)

    def load(slot, chain):
        @pl.when(slot == 0)
        def _():
            for half in range(2):
                st[2 * chain + half] = olds[chain][0, :, half * H : (half + 1) * H]

        @pl.when(jnp.logical_and(slot == 1, jnp.logical_not(can_take(chain))))
        def _():
            for half in range(2):
                st[2 * chain + half] = news[chain][:, half * H : (half + 1) * H]

        @pl.when(jnp.logical_and(slot == 1, can_take(chain)))
        def _():
            for half in range(2):
                hand(chain, half).wait_recv()
                st[2 * chain + half] = land[2 * chain + half]

    plans, landed = [], 0
    for q in range(rounds):
        offset, size = q * H, H if q + 1 < rounds else grad.shape[0] - q * H
        halvings, doublings = [], []
        for s in range(bits):
            bit, other = partner(s)
            give = offset
            if size % 16 == 0:
                size = size // 2
                give = pl.multiple_of(offset + (1 - bit) * size, 8)
                offset = pl.multiple_of(offset + bit * size, 8)
                doublings.insert(0, (other, offset, offset, size, None))
            halvings.append((other, give, offset, size, landed))
            landed += size
        plans.append(halvings + doublings)
    pointer = [0] * rounds

    def piece(q, phase):
        other, give, keep, size, place = plans[q][phase]
        if place is None:
            src, dst = gout.at[pl.ds(give, size)], gout.at[pl.ds(give, size)]
        else:
            src, dst = grad.at[pl.ds(give, size)], gland.at[place : place + size]
        return pltpu.make_async_remote_copy(
            src, dst, gs_sem.at[q, phase], gr_sem.at[q, phase],
            device_id={"dom": other}, device_id_type=MESH,
        )

    def pump(q):
        phase = pointer[q]
        pointer[q] = phase + 1
        if 0 < phase <= len(plans[q]):
            piece(q, phase - 1).wait()
            other, give, keep, size, place = plans[q][phase - 1]
            if place is not None:
                total = grad[pl.ds(keep, size), :] + gland[place : place + size, :]
                if phase == bits:
                    gout[pl.ds(keep, size), :] = total
                else:
                    grad[pl.ds(keep, size), :] = total
        if phase < len(plans[q]):
            piece(q, phase).start()

    emits = (emit_forward, emit_inverse, emit_cotan)
    ends = (end_forward, end_inverse, end_cotan)

    def run_slot(slot, carry):
        pointer[:] = [0] * rounds
        for chain in range(3):
            load(slot, chain)
            emits[chain](0)
        for r in range(rounds):
            for chain in range(3):
                ends[chain](r)
                if r + 1 < rounds:
                    emits[chain](r + 1)
                ready = range(r + 1) if chain == 2 else ()
                if ready:

                    @pl.when(slot == 1)
                    def _():
                        for q in ready:
                            if q + 1 < rounds:
                                pump(q)

                if r >= rounds - 2:
                    store(slot, chain, r % 2 if chain != 1 else 1 - r % 2)
        return carry

    lax.fori_loop(0, 2, run_slot, 0)

    while any(pointer[q] <= len(plans[q]) for q in range(rounds)):
        for q in range(rounds):
            pump(q)
    scale = 1.0 / math.sqrt(2.0 * S * doms)
    for j in range(L):
        for k, (wref, gref) in enumerate(((gwf, ggf), (gws, ggs))):
            index = 2 * j + k
            base = (rounds - 1 - index) * H
            wref[j] = gout[base : base + H, :] * scale
            row = rounds * H + index
            gref[j : j + 1, :] = gout[row : row + 1, :] * scale
    for chain in range(3):
        for half in range(2):
            pl.when(can_send(chain))(lambda c=chain, h=half: hand(c, h).wait_send())


def publish(*refs):
    sems = refs[-1]
    count = len(refs) // 2
    copies = [
        pltpu.make_async_copy(refs[i], refs[count + i], sems.at[i]) for i in range(count)
    ]
    for copy in copies:
        copy.start()
    for copy in copies:
        copy.wait()


def per_device(doms, segs, *args):
    (held, new, bo, bc, bno, bnc, tiles, cols, wf, ws, gf, gs) = args
    S, W = new.shape
    H, L = W // 2, wf.shape[0]
    bits = doms.bit_length() - 1
    rows = 2 * L * H + 8 * doms
    state = jax.ShapeDtypeStruct((1, S, W), F32)
    vmem = pl.BlockSpec(memory_space=pltpu.VMEM)
    results = pl.pallas_call(
        functools.partial(kernel, doms, segs),
        out_shape=[state] * 6
        + [jax.ShapeDtypeStruct((L, H, H), F32)] * 2
        + [jax.ShapeDtypeStruct((L, H), F32)] * 2,
        in_specs=[pl.BlockSpec(memory_space=pltpu.SMEM)] + [vmem] * 11,
        out_specs=[vmem] * 10,
        scratch_shapes=[
            pltpu.VMEM((S, 3 * S), BF16),
            pltpu.VMEM((S, 3 * S), BF16),
            pltpu.VMEM((S, 3 * S), BF16),
            pltpu.VMEM((3 * S, S), BF16),
            pltpu.VMEM((3 * S, S), BF16),
            pltpu.VMEM((2 * L, H, H), BF16),
            pltpu.VMEM((2 * L, H, H), BF16),
            pltpu.VMEM((2 * L, H, H), BF16),
            pltpu.VMEM((6, S, H), F32),
            pltpu.VMEM((2, 2, 3 * S, H), F32),
            pltpu.VMEM((2, 2 * S, H), F32),
            pltpu.VMEM((2, 2 * S, H), F32),
            pltpu.VMEM((S, H), F32),
            pltpu.VMEM((2, S, H), F32),
            pltpu.VMEM((2, S, 1), F32),
            pltpu.VMEM((6, S, H), F32),
            pltpu.VMEM((6, S, H), F32),
            pltpu.VMEM((rows, H), F32),
            pltpu.VMEM((2 * rows, H), F32),
            pltpu.VMEM((rows, H), F32),
            pltpu.SemaphoreType.DMA((3, 2, 2)),
            pltpu.SemaphoreType.DMA((3, 2, 2)),
            pltpu.SemaphoreType.DMA((6,)),
            pltpu.SemaphoreType.DMA((6,)),
            pltpu.SemaphoreType.DMA((2 * L, 2 * bits)),
            pltpu.SemaphoreType.DMA((2 * L, 2 * bits)),
        ],
        compiler_params=pltpu.CompilerParams(
            collective_id=0, has_side_effects=True, vmem_limit_bytes=60 * 1024 * 1024
        ),
    )(cols, held, new, bo, bc, bno, bnc, tiles, wf, ws, gf, gs)
    shapes = [jax.ShapeDtypeStruct(r.shape, r.dtype) for r in results]
    count = len(shapes)
    return tuple(
        pl.pallas_call(
            publish,
            out_shape=shapes,
            in_specs=[vmem] * count,
            out_specs=[pl.BlockSpec(memory_space=pl.ANY)] * count,
            scratch_shapes=[pltpu.SemaphoreType.DMA((count,))],
        )(*results)
    )


def solution(mesh):
    row = P("segment", "dom", None)
    flat = P("dom", None)
    cube = P("segment", None, None)
    vec = P("segment", None)
    return jax.shard_map(
        functools.partial(per_device, mesh.shape["dom"], mesh.shape["segment"]),
        mesh=mesh,
        in_specs=(
            row, flat, row, row, flat, flat,
            P("dom", None, None, None), flat, cube, cube, vec, vec,
        ),
        out_specs=(row,) * 6 + (cube, cube, vec, vec),
        check_vma=False,
    )
```
